32 devices in a mesh: ctx: 8 (over y, x, core), ch: 4 (over z).
Axes of the slice: x: 2, y: 2, z: 4, core: 2. Of those that a mesh axis runs over, the one named last changes fastest.
Arguments:
- latent: bfloat16 [16, 256, 640], P('ctx', 'ch'), may hold values from -6 to 6
- cotangent: bfloat16 [32, 256, 640], P('ctx', 'ch'), may hold values from -6 to 6
- weight: bfloat16 [27, 256, 256], P(None, 'ch'), may hold values from -0.078125 to 0.078125
- clip_ids: int32 [16], replicated, may hold values from 0 to 3, never falling along the last dimension, each value on 1 to 6 neighbouring positions
Outputs:
- grad_latent: bfloat16 [16, 256, 640], P('ctx', 'ch')
- grad_weight: float32 [27, 256, 256], P(None, 'ch', 'ctx')
The draws below stay inside these ranges and needn't reach their ends.
Inputs may be any that keep to these rules, and one draw needn't show every extreme that they name: `clip_ids`: clip ids never fall along the frames; each clip holds 1 to 6 frames and one holds exactly that many.
All inputs are finite; a program needn't handle non-finite values.
Results may differ from the reference program's by a relative error of at most 0.0049.
Values may be sent and summed in bfloat16 or wider, within the bound.
A program may use at most 128 MiB of HBM per device.

```python
import math
import jax
import jax.numpy as jnp
import numpy as np
from jax import lax

C = 256
HB = 4
WW = 160
LAT = 16
TF = 32


def steps_of(stream_key, dims, split, low, high):
    factor_of = 1.0
    for position, shards_of in split:
        heights = jax.random.uniform(jax.random.fold_in(jax.random.fold_in(stream_key, 6), position), (shards_of,), jnp.float32, low / len(split), high / len(split))
        factor_of = factor_of * jnp.repeat(jnp.exp(heights), dims[position] // shards_of).reshape((-1,) + (1,) * (len(dims) - 1 - position))
    return factor_of


def profile(amount, total, most, lean):
    loads = [(1 << 20) // math.isqrt(grade ** lean) + 1 for grade in range(2, amount + 1)]
    rest, holding = total - most - (amount - 1), [1] * (amount - 1)
    while rest > 0:
        candidates = [i for i in range(amount - 1) if holding[i] < most]
        whole, remaining = sum([loads[i] for i in candidates]), rest
        for i in candidates:
            more = min(most - holding[i], max(1, remaining * loads[i] // whole), rest)
            holding[i] = holding[i] + more
            rest = rest - more
    return np.array([most] + holding)


def ragged_sizes(own_key, number_of, total, most, skew):
    if number_of == 2:
        one = jax.random.randint(own_key, (), max(1, total - most), min(most, total - 1) + 1)
        return jnp.stack([one, total - one])
    tallies = jnp.asarray(profile(number_of, total, most, skew), jnp.int32)
    pairs = (number_of - 1) // 2
    source_of, receiver = tallies[1:1 + 2 * pairs:2], tallies[2:2 + 2 * pairs:2]
    slack = jnp.minimum(source_of - 1, most - receiver)
    shifted = jax.random.randint(jax.random.fold_in(own_key, 1), (pairs,), 0, 1 << 20) % (slack + 1)
    tallies = tallies.at[1:1 + 2 * pairs:2].set(source_of - shifted).at[2:2 + 2 * pairs:2].set(receiver + shifted)
    return tallies[jax.random.permutation(jax.random.fold_in(own_key, 2), number_of)]


def noise(key, extent, scale, reach, cuts=(), kind=jnp.bfloat16):
    gain = steps_of(key, extent, cuts, -0.22, 0.18) if cuts else 1.0
    array = jax.random.normal(key, extent, jnp.float32) * scale * gain
    return jnp.minimum(jnp.maximum(array, -reach), reach).astype(kind)


def setup_inputs(seed: int = 0) -> dict:
    keys = jax.random.split(jax.random.key(seed), 5)
    latent = noise(keys[0], (LAT, C, HB * WW), 1.0, 6.0, ((0, 8), (1, 4)))
    cotangent = noise(keys[1], (TF, C, HB * WW), 1.0, 6.0, ((0, 8), (1, 4)))
    weight = noise(keys[2], (27, C, C), (27 * C) ** -0.5, 0.078125, ((1, 4),))
    clip_ids = jnp.searchsorted(jnp.cumsum(ragged_sizes(keys[3], 4, LAT, 3 * LAT // 8, 2)), jnp.arange(LAT), side="right").astype(jnp.int32)
    return dict(latent=latent, cotangent=cotangent, weight=weight, clip_ids=clip_ids)


offsets = [(r_off, c_off) for r_off in (-1, 0, 1) for c_off in (-1, 0, 1)]


def spatial_shift(block, row_step, col_step):
    lead = block.shape[:-1]
    grid = block.reshape(lead + (HB, WW))
    widths = [(0, 0)] * len(lead) + [(1, 1), (1, 1)]
    padded = jnp.pad(grid, widths)
    cut = padded[..., 1 + row_step:1 + row_step + HB, 1 + col_step:1 + col_step + WW]
    return cut.reshape(lead + (HB * WW,))


def delayed(values, lag, fill):
    head = jnp.full((lag,) + values.shape[1:], fill, dtype=values.dtype)
    return jnp.concatenate([head, values[:values.shape[0] - lag]], axis=0)


def advanced(values, lag):
    tail = jnp.zeros((lag,) + values.shape[1:], dtype=values.dtype)
    return jnp.concatenate([values[lag:], tail], axis=0)


def reference(latent, cotangent, weight, clip_ids):
    upsampled = jnp.repeat(latent, 2, axis=0).astype(jnp.float32)
    frame_ids = jnp.repeat(clip_ids, 2).astype(jnp.int32)
    kernel = weight.astype(jnp.float32)
    pre = jnp.zeros(upsampled.shape, jnp.float32)
    for tap_time in range(3):
        keep = (delayed(frame_ids, tap_time, -1) == frame_ids).astype(jnp.float32)
        source = delayed(upsampled, tap_time, 0.0)
        for spot, (row_step, col_step) in enumerate(offsets):
            moved = spatial_shift(source, row_step, col_step)
            pre = pre + keep[:, None, None] * jnp.einsum('oc,tcp->top', kernel[9 * tap_time + spot], moved)
    sig = jax.nn.sigmoid(pre)
    slope = sig * (1.0 + pre * (1.0 - sig))
    grad_pre = (cotangent.astype(jnp.float32) * slope).astype(jnp.bfloat16)
    grad_pre = lax.optimization_barrier(grad_pre).astype(jnp.float32)
    grad_up = jnp.zeros(upsampled.shape, jnp.float32)
    pieces = []
    for tap_time in range(3):
        keep = (delayed(frame_ids, tap_time, -1) == frame_ids).astype(jnp.float32)
        masked = grad_pre * keep[:, None, None]
        source = delayed(upsampled, tap_time, 0.0)
        for spot, (row_step, col_step) in enumerate(offsets):
            back = jnp.einsum('oc,top->tcp', kernel[9 * tap_time + spot], masked)
            back = spatial_shift(back, -row_step, -col_step)
            grad_up = grad_up + advanced(back, tap_time)
            moved = spatial_shift(source, row_step, col_step)
            pieces.append(jnp.einsum('top,tcp->oc', masked, moved))
    grad_latent = (grad_up[0::2] + grad_up[1::2]).astype(jnp.bfloat16)
    grad_weight = jnp.stack(pieces, axis=0)
    return grad_latent, grad_weight
```

```python
import functools

import jax
import jax.numpy as jnp
from jax import lax
from jax.experimental import pallas as pl
from jax.experimental.pallas import tpu as pltpu
from jax.sharding import PartitionSpec as P

HB = 4
WW = 160
CELLS = HB * WW
MESH = pl.DeviceIdType.MESH

offsets = [(r_off, c_off) for r_off in (-1, 0, 1) for c_off in (-1, 0, 1)]


def edge_masks():
    cell = lax.broadcasted_iota(jnp.int32, (1, CELLS), 1)
    row, col = cell // WW, cell % WW
    masks = {}
    for r, c in offsets:
        inside = (row + r >= 0) & (row + r < HB) & (col + c >= 0) & (col + c < WW)
        masks[r, c] = inside.astype(jnp.float32)
    return masks


def moved(value, r, c, masks):
    step = r * WW + c
    if step == 0:
        return value
    return pltpu.roll(value, (-step) % CELLS, 1) * masks[r, c]


def kernel(
    n_ctx, n_ch, ids_ref, latent_ref, cot_ref, w_ref, gl_ref, gw_ref,
    xg, wt, terms, fwd_out, fwd_in, bwd_out, bwd_in, grads, stack, sx, rx, acc, sw, rw,
    gat_send, gat_recv, halo_send, halo_recv, x_send, x_recv, w_send, w_recv,
):
    ctx, ch = lax.axis_index("ctx"), lax.axis_index("ch")
    frames, own = latent_ref.shape[0], latent_ref.shape[1]
    rows = w_ref.shape[0] * own
    width = w_ref.shape[2]
    share = width // n_ctx
    f32, bf16 = jnp.float32, jnp.bfloat16

    for d in range(1, n_ch):
        pl.semaphore_signal(pltpu.get_barrier_semaphore(), inc=1,
                            device_id=(ctx, lax.rem(ch + d, n_ch)), device_id_type=MESH)
    for d in range(1, n_ctx):
        pl.semaphore_signal(pltpu.get_barrier_semaphore(), inc=1,
                            device_id=(lax.rem(ctx + d, n_ctx), ch), device_id_type=MESH)
    for s in range(frames):
        xg[s, ch] = latent_ref[s]
    pl.semaphore_wait(pltpu.get_barrier_semaphore(), n_ch + n_ctx - 2)

    def hop(way, step, s):
        chunk = ch - step if way == 0 else ch + step
        peer = ch + 1 if way == 0 else ch - 1
        return pltpu.make_async_remote_copy(
            src_ref=xg.at[s, chunk], dst_ref=xg.at[s, chunk],
            send_sem=gat_send.at[way, step, s], recv_sem=gat_recv.at[way, step, s],
            device_id=(ctx, peer), device_id_type=MESH)

    def landing(way, step, s):
        chunk = ch - 1 - step if way == 0 else ch + 1 + step
        peer = ch - 1 if way == 0 else ch + 1
        return pltpu.make_async_remote_copy(
            src_ref=xg.at[s, chunk], dst_ref=xg.at[s, chunk],
            send_sem=gat_send.at[way, step, s], recv_sem=gat_recv.at[way, step, s],
            device_id=(ctx, peer), device_id_type=MESH)

    def has(way, step):
        return ch - step >= 0 if way == 0 else ch + step < n_ch

    def sends(way, step):
        if way == 0:
            return (ch - step >= 0) & (ch + 1 < n_ch)
        return (ch + step < n_ch) & (ch >= 1)

    for step in range(n_ch):
        if step == 1:
            wt[...] = jnp.transpose(w_ref[...].reshape(rows, width))
        for s in reversed(range(frames)):
            for way in range(2):
                if step > 0:
                    @pl.when(has(way, step))
                    def _(way=way, step=step, s=s):
                        landing(way, step - 1, s).wait_recv()
                if step < n_ch - 1:
                    @pl.when(sends(way, step))
                    def _(way=way, step=step, s=s):
                        hop(way, step, s).start()

    masks = edge_masks()
    last = frames - 1

    def convolve(s):
        x = xg[s].reshape(width, CELLS)
        for k in range(3):
            prod = jnp.dot(w_ref[9 * k : 9 * k + 9].reshape(9 * own, width), x,
                           preferred_element_type=f32)
            total = None
            for spot, (r, c) in enumerate(offsets):
                part = moved(prod[spot * own : (spot + 1) * own], r, c, masks)
                total = part if total is None else total + part
            terms[s, k] = total

    def fwd_copy():
        return pltpu.make_async_remote_copy(
            src_ref=fwd_out, dst_ref=fwd_in, send_sem=halo_send.at[0], recv_sem=halo_recv.at[0],
            device_id=(lax.rem(ctx + 1, n_ctx), ch), device_id_type=MESH)

    def bwd_copy():
        return pltpu.make_async_remote_copy(
            src_ref=bwd_out, dst_ref=bwd_in, send_sem=halo_send.at[1], recv_sem=halo_recv.at[1],
            device_id=(lax.rem(ctx + n_ctx - 1, n_ctx), ch), device_id_type=MESH)

    convolve(last)
    fwd_out[0] = (terms[last, 1] + terms[last, 2]).astype(bf16)
    fwd_out[1] = terms[last, 2].astype(bf16)

    @pl.when(ctx + 1 < n_ctx)
    def _():
        fwd_copy().start()

    for s in reversed(range(last)):
        convolve(s)

    def same(a, b):
        return (ids_ref[a] == ids_ref[b]).astype(f32)

    base = ctx * frames
    top = n_ctx * frames - 1

    def joined(s):
        low = jnp.maximum(base + s - 1, 0) if s == 0 else base + s - 1
        return same(low, base + s)

    def slopes(s, both, late):
        gate = joined(s)
        for odd in range(2):
            if odd == 0:
                pre = terms[s, 0] + gate * both
            else:
                pre = terms[s, 0] + terms[s, 1] + gate * late
            sig = jax.nn.sigmoid(pre)
            slope = sig * (1.0 + pre * (1.0 - sig))
            grads[2 * s + odd] = (cot_ref[2 * s + odd].astype(f32) * slope).astype(bf16)

    for s in range(1, frames):
        slopes(s, terms[s - 1, 1] + terms[s - 1, 2], terms[s - 1, 2])

    @pl.when(ctx > 0)
    def _():
        fwd_copy().wait_recv()

    @pl.when(ctx == 0)
    def _():
        fwd_in[...] = jnp.zeros_like(fwd_in)

    slopes(0, fwd_in[0].astype(f32), fwd_in[1].astype(f32))
    bwd_out[0] = grads[0]
    bwd_out[1] = (grads[0].astype(f32) + grads[1].astype(f32)).astype(bf16)

    @pl.when(ctx > 0)
    def _():
        bwd_copy().start()

    def x_copy(s, d):
        peer = lax.rem(ch + d, n_ch)
        return pltpu.make_async_remote_copy(
            src_ref=sx.at[s, peer], dst_ref=rx.at[s, d],
            send_sem=x_send.at[s, d], recv_sem=x_recv.at[s, d],
            device_id=(ctx, peer), device_id_type=MESH)

    def w_copy(d):
        peer = lax.rem(ctx + d, n_ctx)
        return pltpu.make_async_remote_copy(
            src_ref=sw.at[peer], dst_ref=rw.at[d],
            send_sem=w_send.at[d], recv_sem=w_recv.at[d],
            device_id=(peer, ch), device_id_type=MESH)

    for s in range(frames):
        if s == last:
            @pl.when(ctx + 1 < n_ctx)
            def _():
                bwd_copy().wait_recv()

            @pl.when(ctx + 1 == n_ctx)
            def _():
                bwd_in[...] = jnp.zeros_like(bwd_in)

            after, pair = bwd_in[0].astype(f32), bwd_in[1].astype(f32)
            gate = same(base + s, jnp.minimum(base + s + 1, top))
        else:
            after = grads[2 * s + 2].astype(f32)
            pair = after + grads[2 * s + 3].astype(f32)
            gate = same(base + s, base + s + 1)
        odd = grads[2 * s + 1].astype(f32)
        groups = [grads[2 * s].astype(f32) + odd, odd + gate * after, gate * pair]
        for k in range(3):
            for spot, (r, c) in enumerate(offsets):
                tap = 9 * k + spot
                stack[s, tap * own : (tap + 1) * own] = moved(groups[k], -r, -c, masks).astype(bf16)
        dx = jnp.dot(wt[...], stack[s], preferred_element_type=f32)
        sx[s] = dx.reshape(n_ch, own, CELLS).astype(bf16)
        for d in range(1, n_ch):
            x_copy(s, d).start()
        x = xg[s].reshape(width, CELLS)
        dw = lax.dot_general(x, stack[s], (((1,), (1,)), ((), ())), preferred_element_type=f32)
        if s == 0:
            acc[...] = dw
        elif s < last:
            acc[...] += dw
        else:
            sw[...] = (acc[...] + dw if frames > 1 else dw).reshape(n_ctx, share, rows).astype(bf16)
    for d in range(1, n_ctx):
        w_copy(d).start()

    for s in range(frames):
        total = sx[s, ch].astype(f32)
        for d in range(1, n_ch):
            x_copy(s, d).wait_recv()
            total = total + rx[s, d].astype(f32)
        gl_ref[s] = total.astype(bf16)
    total = sw[ctx].astype(f32)
    for d in range(1, n_ctx):
        w_copy(d).wait_recv()
        total = total + rw[d].astype(f32)
    gw_ref[...] = jnp.transpose(total).reshape(gw_ref.shape)

    for step in range(n_ch - 1):
        for s in range(frames):
            for way in range(2):
                @pl.when(sends(way, step))
                def _(way=way, step=step, s=s):
                    hop(way, step, s).wait_send()

    @pl.when(ctx + 1 < n_ctx)
    def _():
        fwd_copy().wait_send()

    @pl.when(ctx > 0)
    def _():
        bwd_copy().wait_send()

    for s in range(frames):
        for d in range(1, n_ch):
            x_copy(s, d).wait_send()
    for d in range(1, n_ctx):
        w_copy(d).wait_send()


def on_device(n_ctx, n_ch, latent, cotangent, weight, clip_ids):
    frames, own = latent.shape[:2]
    taps, _, width = weight.shape
    rows, share = taps * own, width // n_ctx
    bf16, f32 = jnp.bfloat16, jnp.float32
    dma = pltpu.SemaphoreType.DMA
    vmem = pl.BlockSpec(memory_space=pltpu.VMEM)
    return pl.pallas_call(
        functools.partial(kernel, n_ctx, n_ch),
        out_shape=(
            jax.ShapeDtypeStruct(latent.shape, bf16),
            jax.ShapeDtypeStruct((taps, own, share), f32),
        ),
        in_specs=[pl.BlockSpec(memory_space=pltpu.SMEM), vmem, vmem, vmem],
        out_specs=(vmem, vmem),
        scratch_shapes=[
            pltpu.VMEM((frames, n_ch, own, CELLS), bf16),
            pltpu.VMEM((width, rows), bf16),
            pltpu.VMEM((frames, 3, own, CELLS), f32),
            pltpu.VMEM((2, own, CELLS), bf16),
            pltpu.VMEM((2, own, CELLS), bf16),
            pltpu.VMEM((2, own, CELLS), bf16),
            pltpu.VMEM((2, own, CELLS), bf16),
            pltpu.VMEM((2 * frames, own, CELLS), bf16),
            pltpu.VMEM((frames, rows, CELLS), bf16),
            pltpu.VMEM((frames, n_ch, own, CELLS), bf16),
            pltpu.VMEM((frames, n_ch, own, CELLS), bf16),
            pltpu.VMEM((width, rows), f32),
            pltpu.VMEM((n_ctx, share, rows), bf16),
            pltpu.VMEM((n_ctx, share, rows), bf16),
            dma((2, n_ch - 1, frames)),
            dma((2, n_ch - 1, frames)),
            dma((2,)),
            dma((2,)),
            dma((frames, n_ch)),
            dma((frames, n_ch)),
            dma((n_ctx,)),
            dma((n_ctx,)),
        ],
        compiler_params=pltpu.CompilerParams(
            collective_id=0, has_side_effects=True, vmem_limit_bytes=48 * 1024 * 1024
        ),
    )(clip_ids, latent, cotangent, weight)


def solution(mesh):
    placed = (P("ctx", "ch", None), P("ctx", "ch", None), P(None, "ch", None), P())
    return jax.shard_map(
        functools.partial(on_device, mesh.shape["ctx"], mesh.shape["ch"]),
        mesh=mesh,
        in_specs=placed,
        out_specs=(P("ctx", "ch", None), P(None, "ch", "ctx")),
        check_vma=False,
    )
```

```python
import functools

import jax
import jax.numpy as jnp
from jax import lax
from jax.experimental import pallas as pl
from jax.experimental.pallas import tpu as pltpu
from jax.sharding import PartitionSpec as P

HB = 4
WW = 160
CELLS = HB * WW
MESH = pl.DeviceIdType.MESH

offsets = [(r_off, c_off) for r_off in (-1, 0, 1) for c_off in (-1, 0, 1)]


def edge_masks():
    cell = lax.broadcasted_iota(jnp.int32, (1, CELLS), 1)
    row, col = cell // WW, cell % WW
    masks = {}
    for r, c in offsets:
        inside = (row + r >= 0) & (row + r < HB) & (col + c >= 0) & (col + c < WW)
        masks[r, c] = inside.astype(jnp.float32)
    return masks


def moved(value, r, c, masks):
    step = r * WW + c
    if step == 0:
        return value
    return pltpu.roll(value, (-step) % CELLS, 1) * masks[r, c]


def kernel(
    n_ctx, n_ch, ids_ref, latent_hbm, cot_hbm, w_hbm, gl_ref, gw_ref,
    w_ref, cot_ref, xg, wt, terms, fwd_out, fwd_in, bwd_out, bwd_in, grads, stack, sx, rx, acc, sw, rw,
    load_sem, gat_send, gat_recv, halo_send, halo_recv, x_send, x_recv, w_send, w_recv,
):
    ctx, ch = lax.axis_index("ctx"), lax.axis_index("ch")
    frames, own = latent_hbm.shape[0], latent_hbm.shape[1]
    rows = w_ref.shape[0] * own
    width = w_ref.shape[2]
    share = width // n_ctx
    f32, bf16 = jnp.float32, jnp.bfloat16

    loads = [
        pltpu.make_async_copy(latent_hbm.at[s], xg.at[s, ch], load_sem.at[s])
        for s in range(frames)
    ]
    loads.append(pltpu.make_async_copy(w_hbm, w_ref, load_sem.at[frames]))
    loads.append(pltpu.make_async_copy(cot_hbm, cot_ref, load_sem.at[frames + 1]))
    for load in reversed(loads[:frames]):
        load.start()
    for load in loads[frames:]:
        load.start()
    for d in range(1, n_ch):
        pl.semaphore_signal(pltpu.get_barrier_semaphore(), inc=1,
                            device_id=(ctx, lax.rem(ch + d, n_ch)), device_id_type=MESH)
    for d in range(1, n_ctx):
        pl.semaphore_signal(pltpu.get_barrier_semaphore(), inc=1,
                            device_id=(lax.rem(ctx + d, n_ctx), ch), device_id_type=MESH)
    pl.semaphore_wait(pltpu.get_barrier_semaphore(), n_ch + n_ctx - 2)

    def hop(way, step, s):
        chunk = ch - step if way == 0 else ch + step
        peer = ch + 1 if way == 0 else ch - 1
        return pltpu.make_async_remote_copy(
            src_ref=xg.at[s, chunk], dst_ref=xg.at[s, chunk],
            send_sem=gat_send.at[way, step, s], recv_sem=gat_recv.at[way, step, s],
            device_id=(ctx, peer), device_id_type=MESH)

    def landing(way, step, s):
        chunk = ch - 1 - step if way == 0 else ch + 1 + step
        peer = ch - 1 if way == 0 else ch + 1
        return pltpu.make_async_remote_copy(
            src_ref=xg.at[s, chunk], dst_ref=xg.at[s, chunk],
            send_sem=gat_send.at[way, step, s], recv_sem=gat_recv.at[way, step, s],
            device_id=(ctx, peer), device_id_type=MESH)

    def has(way, step):
        return ch - step >= 0 if way == 0 else ch + step < n_ch

    def sends(way, step):
        if way == 0:
            return (ch - step >= 0) & (ch + 1 < n_ch)
        return (ch + step < n_ch) & (ch >= 1)

    for step in range(n_ch - 1):
        if step == 1:
            loads[frames].wait()
            wt[...] = jnp.transpose(w_ref[...].reshape(rows, width))
        for s in reversed(range(frames)):
            if step == 0:
                loads[s].wait()
            for way in range(2):
                if step > 0:
                    @pl.when(has(way, step))
                    def _(way=way, step=step, s=s):
                        landing(way, step - 1, s).wait_recv()
                @pl.when(sends(way, step))
                def _(way=way, step=step, s=s):
                    hop(way, step, s).start()

    def gathered(s):
        for way in range(2):
            @pl.when(has(way, n_ch - 1))
            def _(way=way):
                landing(way, n_ch - 2, s).wait_recv()

    masks = edge_masks()
    last = frames - 1

    def convolve(s):
        x = xg[s].reshape(width, CELLS)
        for k in range(3):
            prod = jnp.dot(w_ref[9 * k : 9 * k + 9].reshape(9 * own, width), x,
                           preferred_element_type=f32)
            total = None
            for spot, (r, c) in enumerate(offsets):
                part = moved(prod[spot * own : (spot + 1) * own], r, c, masks)
                total = part if total is None else total + part
            terms[s, k] = total

    def fwd_copy():
        return pltpu.make_async_remote_copy(
            src_ref=fwd_out, dst_ref=fwd_in, send_sem=halo_send.at[0], recv_sem=halo_recv.at[0],
            device_id=(lax.rem(ctx + 1, n_ctx), ch), device_id_type=MESH)

    def bwd_copy():
        return pltpu.make_async_remote_copy(
            src_ref=bwd_out, dst_ref=bwd_in, send_sem=halo_send.at[1], recv_sem=halo_recv.at[1],
            device_id=(lax.rem(ctx + n_ctx - 1, n_ctx), ch), device_id_type=MESH)

    gathered(last)
    convolve(last)
    fwd_out[0] = (terms[last, 1] + terms[last, 2]).astype(bf16)
    fwd_out[1] = terms[last, 2].astype(bf16)

    @pl.when(ctx + 1 < n_ctx)
    def _():
        fwd_copy().start()

    for s in reversed(range(last)):
        gathered(s)
        convolve(s)
    loads[frames + 1].wait()

    def same(a, b):
        return (ids_ref[a] == ids_ref[b]).astype(f32)

    base = ctx * frames
    top = n_ctx * frames - 1

    def joined(s):
        low = jnp.maximum(base + s - 1, 0) if s == 0 else base + s - 1
        return same(low, base + s)

    def slopes(s, both, late):
        gate = joined(s)
        for odd in range(2):
            if odd == 0:
                pre = terms[s, 0] + gate * both
            else:
                pre = terms[s, 0] + terms[s, 1] + gate * late
            sig = jax.nn.sigmoid(pre)
            slope = sig * (1.0 + pre * (1.0 - sig))
            grads[2 * s + odd] = (cot_ref[2 * s + odd].astype(f32) * slope).astype(bf16)

    for s in range(1, frames):
        slopes(s, terms[s - 1, 1] + terms[s - 1, 2], terms[s - 1, 2])

    @pl.when(ctx > 0)
    def _():
        fwd_copy().wait_recv()

    @pl.when(ctx == 0)
    def _():
        fwd_in[...] = jnp.zeros_like(fwd_in)

    slopes(0, fwd_in[0].astype(f32), fwd_in[1].astype(f32))
    bwd_out[0] = grads[0]
    bwd_out[1] = (grads[0].astype(f32) + grads[1].astype(f32)).astype(bf16)

    @pl.when(ctx > 0)
    def _():
        bwd_copy().start()

    def x_copy(s, d):
        peer = lax.rem(ch + d, n_ch)
        return pltpu.make_async_remote_copy(
            src_ref=sx.at[s, peer], dst_ref=rx.at[s, d],
            send_sem=x_send.at[s, d], recv_sem=x_recv.at[s, d],
            device_id=(ctx, peer), device_id_type=MESH)

    def w_copy(d):
        peer = lax.rem(ctx + d, n_ctx)
        return pltpu.make_async_remote_copy(
            src_ref=sw.at[peer], dst_ref=rw.at[d],
            send_sem=w_send.at[d], recv_sem=w_recv.at[d],
            device_id=(peer, ch), device_id_type=MESH)

    for s in range(frames):
        if s == last:
            @pl.when(ctx + 1 < n_ctx)
            def _():
                bwd_copy().wait_recv()

            @pl.when(ctx + 1 == n_ctx)
            def _():
                bwd_in[...] = jnp.zeros_like(bwd_in)

            after, pair = bwd_in[0].astype(f32), bwd_in[1].astype(f32)
            gate = same(base + s, jnp.minimum(base + s + 1, top))
        else:
            after = grads[2 * s + 2].astype(f32)
            pair = after + grads[2 * s + 3].astype(f32)
            gate = same(base + s, base + s + 1)
        odd = grads[2 * s + 1].astype(f32)
        groups = [grads[2 * s].astype(f32) + odd, odd + gate * after, gate * pair]
        for k in range(3):
            for spot, (r, c) in enumerate(offsets):
                tap = 9 * k + spot
                stack[s, tap * own : (tap + 1) * own] = moved(groups[k], -r, -c, masks).astype(bf16)
        dx = jnp.dot(wt[...], stack[s], preferred_element_type=f32)
        sx[s] = dx.reshape(n_ch, own, CELLS).astype(bf16)
        for d in range(1, n_ch):
            x_copy(s, d).start()
        x = xg[s].reshape(width, CELLS)
        dw = lax.dot_general(x, stack[s], (((1,), (1,)), ((), ())), preferred_element_type=f32)
        if s == 0:
            acc[...] = dw
        elif s < last:
            acc[...] += dw
        else:
            sw[...] = (acc[...] + dw if frames > 1 else dw).reshape(n_ctx, share, rows).astype(bf16)
    for d in range(1, n_ctx):
        w_copy(d).start()

    for s in range(frames):
        total = sx[s, ch].astype(f32)
        for d in range(1, n_ch):
            x_copy(s, d).wait_recv()
            total = total + rx[s, d].astype(f32)
        gl_ref[s] = total.astype(bf16)
    total = sw[ctx].astype(f32)
    for d in range(1, n_ctx):
        w_copy(d).wait_recv()
        total = total + rw[d].astype(f32)
    for tap in range(gw_ref.shape[0]):
        gw_ref[tap] = total[:, tap * own : (tap + 1) * own]

    for step in range(n_ch - 1):
        for s in range(frames):
            for way in range(2):
                @pl.when(sends(way, step))
                def _(way=way, step=step, s=s):
                    hop(way, step, s).wait_send()

    @pl.when(ctx + 1 < n_ctx)
    def _():
        fwd_copy().wait_send()

    @pl.when(ctx > 0)
    def _():
        bwd_copy().wait_send()

    for s in range(frames):
        for d in range(1, n_ch):
            x_copy(s, d).wait_send()
    for d in range(1, n_ctx):
        w_copy(d).wait_send()


def on_device(n_ctx, n_ch, latent, cotangent, weight, clip_ids):
    frames, own = latent.shape[:2]
    taps, _, width = weight.shape
    rows, share = taps * own, width // n_ctx
    bf16, f32 = jnp.bfloat16, jnp.float32
    dma = pltpu.SemaphoreType.DMA
    vmem = pl.BlockSpec(memory_space=pltpu.VMEM)
    hbm = pl.BlockSpec(memory_space=pltpu.HBM)
    grad_latent, grad_weight = pl.pallas_call(
        functools.partial(kernel, n_ctx, n_ch),
        out_shape=(
            jax.ShapeDtypeStruct(latent.shape, bf16),
            jax.ShapeDtypeStruct((taps, share, own), f32),
        ),
        in_specs=[pl.BlockSpec(memory_space=pltpu.SMEM), hbm, hbm, hbm],
        out_specs=(vmem, vmem),
        scratch_shapes=[
            pltpu.VMEM(weight.shape, bf16),
            pltpu.VMEM(cotangent.shape, bf16),
            pltpu.VMEM((frames, n_ch, own, CELLS), bf16),
            pltpu.VMEM((width, rows), bf16),
            pltpu.VMEM((frames, 3, own, CELLS), f32),
            pltpu.VMEM((2, own, CELLS), bf16),
            pltpu.VMEM((2, own, CELLS), bf16),
            pltpu.VMEM((2, own, CELLS), bf16),
            pltpu.VMEM((2, own, CELLS), bf16),
            pltpu.VMEM((2 * frames, own, CELLS), bf16),
            pltpu.VMEM((frames, rows, CELLS), bf16),
            pltpu.VMEM((frames, n_ch, own, CELLS), bf16),
            pltpu.VMEM((frames, n_ch, own, CELLS), bf16),
            pltpu.VMEM((width, rows), f32),
            pltpu.VMEM((n_ctx, share, rows), bf16),
            pltpu.VMEM((n_ctx, share, rows), bf16),
            dma((frames + 2,)),
            dma((2, n_ch - 1, frames)),
            dma((2, n_ch - 1, frames)),
            dma((2,)),
            dma((2,)),
            dma((frames, n_ch)),
            dma((frames, n_ch)),
            dma((n_ctx,)),
            dma((n_ctx,)),
        ],
        compiler_params=pltpu.CompilerParams(
            collective_id=0, has_side_effects=True, vmem_limit_bytes=64000 * 1024
        ),
    )(clip_ids, latent, cotangent, weight)
    return grad_latent, jnp.swapaxes(grad_weight, 1, 2)


def solution(mesh):
    placed = (P("ctx", "ch", None), P("ctx", "ch", None), P(None, "ch", None), P())
    return jax.shard_map(
        functools.partial(on_device, mesh.shape["ctx"], mesh.shape["ch"]),
        mesh=mesh,
        in_specs=placed,
        out_specs=(P("ctx", "ch", None), P(None, "ch", "ctx")),
        check_vma=False,
    )
```

```python
import functools

import jax
import jax.numpy as jnp
from jax import lax
from jax.experimental import pallas as pl
from jax.experimental.pallas import tpu as pltpu
from jax.sharding import PartitionSpec as P

HB = 4
WW = 160
CELLS = HB * WW
MESH = pl.DeviceIdType.MESH

offsets = [(r_off, c_off) for r_off in (-1, 0, 1) for c_off in (-1, 0, 1)]


def edge_masks():
    cell = lax.broadcasted_iota(jnp.int32, (1, CELLS), 1)
    row, col = cell // WW, cell % WW
    masks = {}
    for r, c in offsets:
        inside = (row + r >= 0) & (row + r < HB) & (col + c >= 0) & (col + c < WW)
        masks[r, c] = inside.astype(jnp.float32)
    return masks


def moved(value, r, c, masks):
    step = r * WW + c
    if step == 0:
        return value
    return pltpu.roll(value, (-step) % CELLS, 1) * masks[r, c]


def kernel(
    n_ctx, n_ch, ids_ref, latent_hbm, cot_hbm, w_hbm, gl_ref, gw_ref,
    w_ref, cot_ref, xg, wt, terms, fwd_out, fwd_in, bwd_out, bwd_in, grads, stack, sx, rx, acc, sw, rw,
    load_sem, gat_send, gat_recv, halo_send, halo_recv, x_send, x_recv, w_send, w_recv,
):
    ctx, ch = lax.axis_index("ctx"), lax.axis_index("ch")
    frames, own = latent_hbm.shape[0], latent_hbm.shape[1]
    rows = w_ref.shape[0] * own
    width = w_ref.shape[2]
    share = width // n_ctx
    f32, bf16 = jnp.float32, jnp.bfloat16

    loads = [
        pltpu.make_async_copy(latent_hbm.at[s], xg.at[s, ch], load_sem.at[s])
        for s in range(frames)
    ]
    loads.append(pltpu.make_async_copy(w_hbm, w_ref, load_sem.at[frames]))
    loads.append(pltpu.make_async_copy(cot_hbm, cot_ref, load_sem.at[frames + 1]))
    for load in reversed(loads[:frames]):
        load.start()
    for load in loads[frames:]:
        load.start()
    for d in range(1, n_ch):
        pl.semaphore_signal(pltpu.get_barrier_semaphore(), inc=1,
                            device_id=(ctx, lax.rem(ch + d, n_ch)), device_id_type=MESH)
    for d in range(1, n_ctx):
        pl.semaphore_signal(pltpu.get_barrier_semaphore(), inc=1,
                            device_id=(lax.rem(ctx + d, n_ctx), ch), device_id_type=MESH)
    pl.semaphore_wait(pltpu.get_barrier_semaphore(), n_ch + n_ctx - 2)

    ways = ((0, 1), (1, -1))
    last = frames - 1

    def inside(place):
        return (place >= 0) & (place < n_ch)

    def hop(way, sign, d, s):
        chunk = ch - sign if d == 2 else ch
        return pltpu.make_async_remote_copy(
            src_ref=xg.at[s, chunk], dst_ref=xg.at[s, chunk],
            send_sem=gat_send.at[way, d - 1, s], recv_sem=gat_recv.at[way, d - 1, s],
            device_id=(ctx, ch + sign if d == 2 else ch + sign * d), device_id_type=MESH)

    def landing(way, sign, d, s):
        chunk = ch - sign * d
        return pltpu.make_async_remote_copy(
            src_ref=xg.at[s, chunk], dst_ref=xg.at[s, chunk],
            send_sem=gat_send.at[way, d - 1, s], recv_sem=gat_recv.at[way, d - 1, s],
            device_id=(ctx, ch - sign), device_id_type=MESH)

    def hops(sign, d):
        return inside(ch - sign) & inside(ch + sign) if d == 2 else inside(ch + sign * d)

    direct = [1] + list(range(3, n_ch))
    for s in reversed(range(frames)):
        loads[s].wait()
        for d in direct:
            for way, sign in ways:
                @pl.when(hops(sign, d))
                def _(way=way, sign=sign, d=d, s=s):
                    hop(way, sign, d, s).start()
    loads[frames].wait()
    wt[...] = jnp.transpose(w_ref[...].reshape(rows, width))
    for s in reversed(range(frames)):
        for way, sign in ways:
            @pl.when(inside(ch - sign))
            def _(way=way, sign=sign, s=s):
                landing(way, sign, 1, s).wait_recv()

            @pl.when(hops(sign, 2))
            def _(way=way, sign=sign, s=s):
                hop(way, sign, 2, s).start()

    def gathered(s):
        for d in range(2, n_ch):
            for way, sign in ways:
                @pl.when(inside(ch - sign * d))
                def _(way=way, sign=sign, d=d):
                    landing(way, sign, d, s).wait_recv()

    masks = edge_masks()

    def convolve(s):
        x = xg[s].reshape(width, CELLS)
        for k in range(3):
            prod = jnp.dot(w_ref[9 * k : 9 * k + 9].reshape(9 * own, width), x,
                           preferred_element_type=f32)
            total = None
            for spot, (r, c) in enumerate(offsets):
                part = moved(prod[spot * own : (spot + 1) * own], r, c, masks)
                total = part if total is None else total + part
            terms[s, k] = total

    def fwd_copy():
        return pltpu.make_async_remote_copy(
            src_ref=fwd_out, dst_ref=fwd_in, send_sem=halo_send.at[0], recv_sem=halo_recv.at[0],
            device_id=(lax.rem(ctx + 1, n_ctx), ch), device_id_type=MESH)

    def bwd_copy():
        return pltpu.make_async_remote_copy(
            src_ref=bwd_out, dst_ref=bwd_in, send_sem=halo_send.at[1], recv_sem=halo_recv.at[1],
            device_id=(lax.rem(ctx + n_ctx - 1, n_ctx), ch), device_id_type=MESH)

    gathered(last)
    convolve(last)
    fwd_out[0] = (terms[last, 1] + terms[last, 2]).astype(bf16)
    fwd_out[1] = terms[last, 2].astype(bf16)

    @pl.when(ctx + 1 < n_ctx)
    def _():
        fwd_copy().start()

    for s in reversed(range(last)):
        gathered(s)
        convolve(s)
    loads[frames + 1].wait()

    def same(a, b):
        return (ids_ref[a] == ids_ref[b]).astype(f32)

    base = ctx * frames
    top = n_ctx * frames - 1

    def joined(s):
        low = jnp.maximum(base + s - 1, 0) if s == 0 else base + s - 1
        return same(low, base + s)

    def slopes(s, both, late):
        gate = joined(s)
        for odd in range(2):
            if odd == 0:
                pre = terms[s, 0] + gate * both
            else:
                pre = terms[s, 0] + terms[s, 1] + gate * late
            sig = jax.nn.sigmoid(pre)
            slope = sig * (1.0 + pre * (1.0 - sig))
            grads[2 * s + odd] = (cot_ref[2 * s + odd].astype(f32) * slope).astype(bf16)

    for s in range(1, frames):
        slopes(s, terms[s - 1, 1] + terms[s - 1, 2], terms[s - 1, 2])

    @pl.when(ctx > 0)
    def _():
        fwd_copy().wait_recv()

    @pl.when(ctx == 0)
    def _():
        fwd_in[...] = jnp.zeros_like(fwd_in)

    slopes(0, fwd_in[0].astype(f32), fwd_in[1].astype(f32))
    bwd_out[0] = grads[0]
    bwd_out[1] = (grads[0].astype(f32) + grads[1].astype(f32)).astype(bf16)

    @pl.when(ctx > 0)
    def _():
        bwd_copy().start()

    def x_copy(way, sign, d, s):
        return pltpu.make_async_remote_copy(
            src_ref=sx.at[s, ch + sign * d], dst_ref=rx.at[s, way, d - 1],
            send_sem=x_send.at[s, way, d - 1], recv_sem=x_recv.at[s, way, d - 1],
            device_id=(ctx, ch + sign if d == 2 else ch + sign * d), device_id_type=MESH)

    def x_landing(way, sign, d, s):
        return pltpu.make_async_remote_copy(
            src_ref=rx.at[s, way, d - 1], dst_ref=rx.at[s, way, d - 1],
            send_sem=x_send.at[s, way, d - 1], recv_sem=x_recv.at[s, way, d - 1],
            device_id=(ctx, ch - sign), device_id_type=MESH)

    def x_start(s):
        for d in range(2, n_ch):
            for way, sign in ways:
                @pl.when(inside(ch + sign * d))
                def _(way=way, sign=sign, d=d):
                    x_copy(way, sign, d, s).start()

    def x_relay(s):
        for way, sign in ways:
            @pl.when(hops(sign, 2))
            def _(way=way, sign=sign):
                x_landing(way, sign, 2, s).wait_recv()
                both = sx[s, ch + sign].astype(f32) + rx[s, way, 1].astype(f32)
                sx[s, ch + sign] = both.astype(bf16)

            @pl.when(inside(ch + sign))
            def _(way=way, sign=sign):
                x_copy(way, sign, 1, s).start()

    def w_copy(d):
        peer = lax.rem(ctx + d, n_ctx)
        return pltpu.make_async_remote_copy(
            src_ref=sw.at[peer], dst_ref=rw.at[d],
            send_sem=w_send.at[d], recv_sem=w_recv.at[d],
            device_id=(peer, ch), device_id_type=MESH)

    for s in range(frames):
        if s == last:
            @pl.when(ctx + 1 < n_ctx)
            def _():
                bwd_copy().wait_recv()

            @pl.when(ctx + 1 == n_ctx)
            def _():
                bwd_in[...] = jnp.zeros_like(bwd_in)

            after, pair = bwd_in[0].astype(f32), bwd_in[1].astype(f32)
            gate = same(base + s, jnp.minimum(base + s + 1, top))
        else:
            after = grads[2 * s + 2].astype(f32)
            pair = after + grads[2 * s + 3].astype(f32)
            gate = same(base + s, base + s + 1)
        odd = grads[2 * s + 1].astype(f32)
        groups = [grads[2 * s].astype(f32) + odd, odd + gate * after, gate * pair]
        for k in range(3):
            for spot, (r, c) in enumerate(offsets):
                tap = 9 * k + spot
                stack[s, tap * own : (tap + 1) * own] = moved(groups[k], -r, -c, masks).astype(bf16)
        dx = jnp.dot(wt[...], stack[s], preferred_element_type=f32)
        sx[s] = dx.reshape(n_ch, own, CELLS).astype(bf16)
        x_start(s)
        if s > 0:
            x_relay(s - 1)
        x = xg[s].reshape(width, CELLS)
        dw = lax.dot_general(x, stack[s], (((1,), (1,)), ((), ())), preferred_element_type=f32)
        if s == 0:
            acc[...] = dw
        elif s < last:
            acc[...] += dw
        else:
            sw[...] = (acc[...] + dw if frames > 1 else dw).reshape(n_ctx, share, rows).astype(bf16)
    for d in range(1, n_ctx):
        w_copy(d).start()
    x_relay(last)

    for s in range(frames):
        terms[s, 0] = sx[s, ch].astype(f32)
        for d in reversed(direct):
            for way, sign in ways:
                @pl.when(inside(ch - sign * d))
                def _(way=way, sign=sign, d=d, s=s):
                    x_landing(way, sign, d, s).wait_recv()
                    terms[s, 0] += rx[s, way, d - 1].astype(f32)

        gl_ref[s] = terms[s, 0].astype(bf16)
    total = sw[ctx].astype(f32)
    for d in range(1, n_ctx):
        w_copy(d).wait_recv()
        total = total + rw[d].astype(f32)
    for tap in range(gw_ref.shape[0]):
        gw_ref[tap] = total[:, tap * own : (tap + 1) * own]

    for s in range(frames):
        for d in range(1, n_ch):
            for way, sign in ways:
                @pl.when(hops(sign, d))
                def _(way=way, sign=sign, d=d, s=s):
                    hop(way, sign, d, s).wait_send()

                @pl.when(inside(ch + sign * d))
                def _(way=way, sign=sign, d=d, s=s):
                    x_copy(way, sign, d, s).wait_send()

    @pl.when(ctx + 1 < n_ctx)
    def _():
        fwd_copy().wait_send()

    @pl.when(ctx > 0)
    def _():
        bwd_copy().wait_send()

    for d in range(1, n_ctx):
        w_copy(d).wait_send()


def on_device(n_ctx, n_ch, latent, cotangent, weight, clip_ids):
    frames, own = latent.shape[:2]
    taps, _, width = weight.shape
    rows, share = taps * own, width // n_ctx
    bf16, f32 = jnp.bfloat16, jnp.float32
    dma = pltpu.SemaphoreType.DMA
    vmem = pl.BlockSpec(memory_space=pltpu.VMEM)
    hbm = pl.BlockSpec(memory_space=pltpu.HBM)
    grad_latent, grad_weight = pl.pallas_call(
        functools.partial(kernel, n_ctx, n_ch),
        out_shape=(
            jax.ShapeDtypeStruct(latent.shape, bf16),
            jax.ShapeDtypeStruct((taps, share, own), f32),
        ),
        in_specs=[pl.BlockSpec(memory_space=pltpu.SMEM), hbm, hbm, hbm],
        out_specs=(vmem, vmem),
        scratch_shapes=[
            pltpu.VMEM(weight.shape, bf16),
            pltpu.VMEM(cotangent.shape, bf16),
            pltpu.VMEM((frames, n_ch, own, CELLS), bf16),
            pltpu.VMEM((width, rows), bf16),
            pltpu.VMEM((frames, 3, own, CELLS), f32),
            pltpu.VMEM((2, own, CELLS), bf16),
            pltpu.VMEM((2, own, CELLS), bf16),
            pltpu.VMEM((2, own, CELLS), bf16),
            pltpu.VMEM((2, own, CELLS), bf16),
            pltpu.VMEM((2 * frames, own, CELLS), bf16),
            pltpu.VMEM((frames, rows, CELLS), bf16),
            pltpu.VMEM((frames, n_ch, own, CELLS), bf16),
            pltpu.VMEM((frames, 2, n_ch - 1, own, CELLS), bf16),
            pltpu.VMEM((width, rows), f32),
            pltpu.VMEM((n_ctx, share, rows), bf16),
            pltpu.VMEM((n_ctx, share, rows), bf16),
            dma((frames + 2,)),
            dma((2, n_ch - 1, frames)),
            dma((2, n_ch - 1, frames)),
            dma((2,)),
            dma((2,)),
            dma((frames, 2, n_ch - 1)),
            dma((frames, 2, n_ch - 1)),
            dma((n_ctx,)),
            dma((n_ctx,)),
        ],
        compiler_params=pltpu.CompilerParams(
            collective_id=0, has_side_effects=True, vmem_limit_bytes=64000 * 1024
        ),
    )(clip_ids, latent, cotangent, weight)
    return grad_latent, jnp.swapaxes(grad_weight, 1, 2)


def solution(mesh):
    placed = (P("ctx", "ch", None), P("ctx", "ch", None), P(None, "ch", None), P())
    return jax.shard_map(
        functools.partial(on_device, mesh.shape["ctx"], mesh.shape["ch"]),
        mesh=mesh,
        in_specs=placed,
        out_specs=(P("ctx", "ch", None), P(None, "ch", "ctx")),
        check_vma=False,
    )
```

```python
import functools

import jax
import jax.numpy as jnp
from jax import lax
from jax.experimental import pallas as pl
from jax.experimental.pallas import tpu as pltpu
from jax.sharding import PartitionSpec as P

HB = 4
WW = 160
CELLS = HB * WW
MESH = pl.DeviceIdType.MESH

offsets = [(r_off, c_off) for r_off in (-1, 0, 1) for c_off in (-1, 0, 1)]


def edge_masks():
    cell = lax.broadcasted_iota(jnp.int32, (1, CELLS), 1)
    row, col = cell // WW, cell % WW
    masks = {}
    for r, c in offsets:
        inside = (row + r >= 0) & (row + r < HB) & (col + c >= 0) & (col + c < WW)
        masks[r, c] = inside.astype(jnp.float32)
    return masks


def moved(value, r, c, masks):
    step = r * WW + c
    if step == 0:
        return value
    return pltpu.roll(value, (-step) % CELLS, 1) * masks[r, c]


def kernel(
    n_ctx, n_ch, ids_ref, latent_hbm, cot_hbm, w_hbm, gl_ref, gw_ref,
    w_ref, cot_ref, xg, wt, terms, fwd_out, fwd_in, bwd_out, bwd_in, grads, stack, sx, rx, acc, sw, rc, rw,
    load_sem, gat_send, gat_recv, halo_send, halo_recv, x_send, x_recv, c_send, c_recv, w_send, w_recv,
):
    ctx, ch = lax.axis_index("ctx"), lax.axis_index("ch")
    frames, own = latent_hbm.shape[0], latent_hbm.shape[1]
    rows = w_ref.shape[0] * own
    width = w_ref.shape[2]
    share = width // n_ctx
    f32, bf16 = jnp.float32, jnp.bfloat16

    loads = [
        pltpu.make_async_copy(latent_hbm.at[s], xg.at[s, ch], load_sem.at[s])
        for s in range(frames)
    ]
    loads.append(pltpu.make_async_copy(w_hbm, w_ref, load_sem.at[frames]))
    loads.append(pltpu.make_async_copy(cot_hbm, cot_ref, load_sem.at[frames + 1]))
    for load in reversed(loads[:frames]):
        load.start()
    for load in loads[frames:]:
        load.start()
    for d in range(1, n_ch):
        pl.semaphore_signal(pltpu.get_barrier_semaphore(), inc=1,
                            device_id=(ctx, lax.rem(ch + d, n_ch)), device_id_type=MESH)
    for d in range(1, n_ctx):
        pl.semaphore_signal(pltpu.get_barrier_semaphore(), inc=1,
                            device_id=(lax.rem(ctx + d, n_ctx), ch), device_id_type=MESH)
    pl.semaphore_wait(pltpu.get_barrier_semaphore(), n_ch + n_ctx - 2)

    ways = ((0, 1), (1, -1))
    last = frames - 1

    def inside(place):
        return (place >= 0) & (place < n_ch)

    def hop(way, sign, d, s):
        chunk = ch - sign if d == 2 else ch
        return pltpu.make_async_remote_copy(
            src_ref=xg.at[s, chunk], dst_ref=xg.at[s, chunk],
            send_sem=gat_send.at[way, d - 1, s], recv_sem=gat_recv.at[way, d - 1, s],
            device_id=(ctx, ch + sign if d == 2 else ch + sign * d), device_id_type=MESH)

    def landing(way, sign, d, s):
        chunk = ch - sign * d
        return pltpu.make_async_remote_copy(
            src_ref=xg.at[s, chunk], dst_ref=xg.at[s, chunk],
            send_sem=gat_send.at[way, d - 1, s], recv_sem=gat_recv.at[way, d - 1, s],
            device_id=(ctx, ch - sign), device_id_type=MESH)

    def hops(sign, d):
        return inside(ch - sign) & inside(ch + sign) if d == 2 else inside(ch + sign * d)

    direct = [1] + list(range(3, n_ch))
    for s in reversed(range(frames)):
        loads[s].wait()
        for d in direct:
            for way, sign in ways:
                @pl.when(hops(sign, d))
                def _(way=way, sign=sign, d=d, s=s):
                    hop(way, sign, d, s).start()
    loads[frames].wait()
    wt[...] = jnp.transpose(w_ref[...].reshape(rows, width))
    for s in reversed(range(frames)):
        for way, sign in ways:
            @pl.when(inside(ch - sign))
            def _(way=way, sign=sign, s=s):
                landing(way, sign, 1, s).wait_recv()

            @pl.when(hops(sign, 2))
            def _(way=way, sign=sign, s=s):
                hop(way, sign, 2, s).start()

    def gathered(s):
        for d in range(2, n_ch):
            for way, sign in ways:
                @pl.when(inside(ch - sign * d))
                def _(way=way, sign=sign, d=d):
                    landing(way, sign, d, s).wait_recv()

    masks = edge_masks()

    def convolve(s):
        x = xg[s].reshape(width, CELLS)
        for k in range(3):
            prod = jnp.dot(w_ref[9 * k : 9 * k + 9].reshape(9 * own, width), x,
                           preferred_element_type=f32)
            total = None
            for spot, (r, c) in enumerate(offsets):
                part = moved(prod[spot * own : (spot + 1) * own], r, c, masks)
                total = part if total is None else total + part
            terms[s, k] = total

    def fwd_copy():
        return pltpu.make_async_remote_copy(
            src_ref=fwd_out, dst_ref=fwd_in, send_sem=halo_send.at[0], recv_sem=halo_recv.at[0],
            device_id=(lax.rem(ctx + 1, n_ctx), ch), device_id_type=MESH)

    def bwd_copy():
        return pltpu.make_async_remote_copy(
            src_ref=bwd_out, dst_ref=bwd_in, send_sem=halo_send.at[1], recv_sem=halo_recv.at[1],
            device_id=(lax.rem(ctx + n_ctx - 1, n_ctx), ch), device_id_type=MESH)

    gathered(last)
    convolve(last)
    fwd_out[0] = (terms[last, 1] + terms[last, 2]).astype(bf16)
    fwd_out[1] = terms[last, 2].astype(bf16)

    @pl.when(ctx + 1 < n_ctx)
    def _():
        fwd_copy().start()

    for s in reversed(range(last)):
        gathered(s)
        convolve(s)
    loads[frames + 1].wait()

    def same(a, b):
        return (ids_ref[a] == ids_ref[b]).astype(f32)

    base = ctx * frames
    top = n_ctx * frames - 1

    def joined(s):
        low = jnp.maximum(base + s - 1, 0) if s == 0 else base + s - 1
        return same(low, base + s)

    def slopes(s, both, late):
        gate = joined(s)
        for odd in range(2):
            if odd == 0:
                pre = terms[s, 0] + gate * both
            else:
                pre = terms[s, 0] + terms[s, 1] + gate * late
            sig = jax.nn.sigmoid(pre)
            slope = sig * (1.0 + pre * (1.0 - sig))
            grads[2 * s + odd] = (cot_ref[2 * s + odd].astype(f32) * slope).astype(bf16)

    for s in range(1, frames):
        slopes(s, terms[s - 1, 1] + terms[s - 1, 2], terms[s - 1, 2])

    @pl.when(ctx > 0)
    def _():
        fwd_copy().wait_recv()

    @pl.when(ctx == 0)
    def _():
        fwd_in[...] = jnp.zeros_like(fwd_in)

    slopes(0, fwd_in[0].astype(f32), fwd_in[1].astype(f32))
    bwd_out[0] = grads[0]
    bwd_out[1] = (grads[0].astype(f32) + grads[1].astype(f32)).astype(bf16)

    @pl.when(ctx > 0)
    def _():
        bwd_copy().start()

    def x_copy(way, sign, d, s):
        return pltpu.make_async_remote_copy(
            src_ref=sx.at[s, ch + sign * d], dst_ref=rx.at[s, way, d - 1],
            send_sem=x_send.at[s, way, d - 1], recv_sem=x_recv.at[s, way, d - 1],
            device_id=(ctx, ch + sign if d == 2 else ch + sign * d), device_id_type=MESH)

    def x_landing(way, sign, d, s):
        return pltpu.make_async_remote_copy(
            src_ref=rx.at[s, way, d - 1], dst_ref=rx.at[s, way, d - 1],
            send_sem=x_send.at[s, way, d - 1], recv_sem=x_recv.at[s, way, d - 1],
            device_id=(ctx, ch - sign), device_id_type=MESH)

    def x_start(s):
        for d in range(2, n_ch):
            for way, sign in ways:
                @pl.when(inside(ch + sign * d))
                def _(way=way, sign=sign, d=d):
                    x_copy(way, sign, d, s).start()

    def x_relay(s):
        for way, sign in ways:
            @pl.when(hops(sign, 2))
            def _(way=way, sign=sign):
                x_landing(way, sign, 2, s).wait_recv()
                both = sx[s, ch + sign].astype(f32) + rx[s, way, 1].astype(f32)
                sx[s, ch + sign] = both.astype(bf16)

            @pl.when(inside(ch + sign))
            def _(way=way, sign=sign):
                x_copy(way, sign, 1, s).start()

    half = n_ctx // 2
    side, pair_at = lax.rem(ctx, 2), ctx // 2

    def core_copy(q):
        return pltpu.make_async_remote_copy(
            src_ref=sw.at[1 - side, q], dst_ref=rc.at[q],
            send_sem=c_send.at[q], recv_sem=c_recv.at[q],
            device_id=(ctx + 1 - 2 * side, ch), device_id_type=MESH)

    def w_copy(d):
        q = lax.rem(pair_at + d, half)
        return pltpu.make_async_remote_copy(
            src_ref=sw.at[side, q], dst_ref=rw.at[d],
            send_sem=w_send.at[d], recv_sem=w_recv.at[d],
            device_id=(2 * q + side, ch), device_id_type=MESH)

    for s in range(frames):
        if s == last:
            @pl.when(ctx + 1 < n_ctx)
            def _():
                bwd_copy().wait_recv()

            @pl.when(ctx + 1 == n_ctx)
            def _():
                bwd_in[...] = jnp.zeros_like(bwd_in)

            after, pair = bwd_in[0].astype(f32), bwd_in[1].astype(f32)
            gate = same(base + s, jnp.minimum(base + s + 1, top))
        else:
            after = grads[2 * s + 2].astype(f32)
            pair = after + grads[2 * s + 3].astype(f32)
            gate = same(base + s, base + s + 1)
        odd = grads[2 * s + 1].astype(f32)
        groups = [grads[2 * s].astype(f32) + odd, odd + gate * after, gate * pair]
        for k in range(3):
            for spot, (r, c) in enumerate(offsets):
                tap = 9 * k + spot
                stack[s, tap * own : (tap + 1) * own] = moved(groups[k], -r, -c, masks).astype(bf16)
        dx = jnp.dot(wt[...], stack[s], preferred_element_type=f32)
        sx[s] = dx.reshape(n_ch, own, CELLS).astype(bf16)
        x_start(s)
        if s > 0:
            x_relay(s - 1)
        x = xg[s].reshape(width, CELLS)
        dw = lax.dot_general(x, stack[s], (((1,), (1,)), ((), ())), preferred_element_type=f32)
        if s == 0:
            acc[...] = dw
        elif s < last:
            acc[...] += dw
        else:
            full = (acc[...] + dw if frames > 1 else dw).reshape(half, 2, share, rows)
            for p in range(2):
                sw[p] = full[:, p].astype(bf16)
    for q in range(half):
        core_copy(q).start()
    x_relay(last)
    for q in range(half):
        core_copy(q).wait_recv()
        sw[side, q] = (sw[side, q].astype(f32) + rc[q].astype(f32)).astype(bf16)
    for d in range(1, half):
        w_copy(d).start()

    for s in range(frames):
        terms[s, 0] = sx[s, ch].astype(f32)
        for d in reversed(direct):
            for way, sign in ways:
                @pl.when(inside(ch - sign * d))
                def _(way=way, sign=sign, d=d, s=s):
                    x_landing(way, sign, d, s).wait_recv()
                    terms[s, 0] += rx[s, way, d - 1].astype(f32)

        gl_ref[s] = terms[s, 0].astype(bf16)
    total = sw[side, pair_at].astype(f32)
    for d in range(1, half):
        w_copy(d).wait_recv()
        total = total + rw[d].astype(f32)
    for tap in range(gw_ref.shape[0]):
        gw_ref[tap] = total[:, tap * own : (tap + 1) * own]

    for s in range(frames):
        for d in range(1, n_ch):
            for way, sign in ways:
                @pl.when(hops(sign, d))
                def _(way=way, sign=sign, d=d, s=s):
                    hop(way, sign, d, s).wait_send()

                @pl.when(inside(ch + sign * d))
                def _(way=way, sign=sign, d=d, s=s):
                    x_copy(way, sign, d, s).wait_send()

    @pl.when(ctx + 1 < n_ctx)
    def _():
        fwd_copy().wait_send()

    @pl.when(ctx > 0)
    def _():
        bwd_copy().wait_send()

    for q in range(half):
        core_copy(q).wait_send()
    for d in range(1, half):
        w_copy(d).wait_send()


def on_device(n_ctx, n_ch, latent, cotangent, weight, clip_ids):
    frames, own = latent.shape[:2]
    taps, _, width = weight.shape
    rows, share = taps * own, width // n_ctx
    bf16, f32 = jnp.bfloat16, jnp.float32
    dma = pltpu.SemaphoreType.DMA
    vmem = pl.BlockSpec(memory_space=pltpu.VMEM)
    hbm = pl.BlockSpec(memory_space=pltpu.HBM)
    grad_latent, grad_weight = pl.pallas_call(
        functools.partial(kernel, n_ctx, n_ch),
        out_shape=(
            jax.ShapeDtypeStruct(latent.shape, bf16),
            jax.ShapeDtypeStruct((taps, share, own), f32),
        ),
        in_specs=[pl.BlockSpec(memory_space=pltpu.SMEM), hbm, hbm, hbm],
        out_specs=(vmem, vmem),
        scratch_shapes=[
            pltpu.VMEM(weight.shape, bf16),
            pltpu.VMEM(cotangent.shape, bf16),
            pltpu.VMEM((frames, n_ch, own, CELLS), bf16),
            pltpu.VMEM((width, rows), bf16),
            pltpu.VMEM((frames, 3, own, CELLS), f32),
            pltpu.VMEM((2, own, CELLS), bf16),
            pltpu.VMEM((2, own, CELLS), bf16),
            pltpu.VMEM((2, own, CELLS), bf16),
            pltpu.VMEM((2, own, CELLS), bf16),
            pltpu.VMEM((2 * frames, own, CELLS), bf16),
            pltpu.VMEM((frames, rows, CELLS), bf16),
            pltpu.VMEM((frames, n_ch, own, CELLS), bf16),
            pltpu.VMEM((frames, 2, n_ch - 1, own, CELLS), bf16),
            pltpu.VMEM((width, rows), f32),
            pltpu.VMEM((2, n_ctx // 2, share, rows), bf16),
            pltpu.VMEM((n_ctx // 2, share, rows), bf16),
            pltpu.VMEM((n_ctx // 2, share, rows), bf16),
            dma((frames + 2,)),
            dma((2, n_ch - 1, frames)),
            dma((2, n_ch - 1, frames)),
            dma((2,)),
            dma((2,)),
            dma((frames, 2, n_ch - 1)),
            dma((frames, 2, n_ch - 1)),
            dma((n_ctx // 2,)),
            dma((n_ctx // 2,)),
            dma((n_ctx // 2,)),
            dma((n_ctx // 2,)),
        ],
        compiler_params=pltpu.CompilerParams(
            collective_id=0, has_side_effects=True, vmem_limit_bytes=64000 * 1024
        ),
    )(clip_ids, latent, cotangent, weight)
    return grad_latent, jnp.swapaxes(grad_weight, 1, 2)


def solution(mesh):
    placed = (P("ctx", "ch", None), P("ctx", "ch", None), P(None, "ch", None), P())
    return jax.shard_map(
        functools.partial(on_device, mesh.shape["ctx"], mesh.shape["ch"]),
        mesh=mesh,
        in_specs=placed,
        out_specs=(P("ctx", "ch", None), P(None, "ch", "ctx")),
        check_vma=False,
    )
```

```python
import functools

import jax
import jax.numpy as jnp
from jax import lax
from jax.experimental import pallas as pl
from jax.experimental.pallas import tpu as pltpu
from jax.sharding import PartitionSpec as P

HB = 4
WW = 160
CELLS = HB * WW
MESH = pl.DeviceIdType.MESH

offsets = [(r_off, c_off) for r_off in (-1, 0, 1) for c_off in (-1, 0, 1)]


def edge_masks():
    cell = lax.broadcasted_iota(jnp.int32, (1, CELLS), 1)
    row, col = cell // WW, cell % WW
    masks = {}
    for r, c in offsets:
        inside = (row + r >= 0) & (row + r < HB) & (col + c >= 0) & (col + c < WW)
        masks[r, c] = inside.astype(jnp.float32)
    return masks


def moved(value, r, c, masks):
    step = r * WW + c
    if step == 0:
        return value
    return pltpu.roll(value, (-step) % CELLS, 1) * masks[r, c]


def kernel(
    n_ctx, n_ch, ids_ref, latent_hbm, cot_hbm, w_hbm, gl_ref, gw_ref,
    w_ref, cot_ref, xg, wt, terms, fwd_out, fwd_in, bwd_out, bwd_in, grads, stack, sx, rx, acc, sw, rc, rw,
    load_sem, gat_send, gat_recv, halo_send, halo_recv, x_send, x_recv, c_send, c_recv, w_send, w_recv,
):
    ctx, ch = lax.axis_index("ctx"), lax.axis_index("ch")
    frames, own = latent_hbm.shape[0], latent_hbm.shape[1]
    rows = w_ref.shape[0] * own
    width = w_ref.shape[2]
    share = width // n_ctx
    f32, bf16 = jnp.float32, jnp.bfloat16

    loads = [
        pltpu.make_async_copy(latent_hbm.at[s], xg.at[s, ch], load_sem.at[s])
        for s in range(frames)
    ]
    loads.append(pltpu.make_async_copy(w_hbm, w_ref, load_sem.at[frames]))
    loads.append(pltpu.make_async_copy(cot_hbm, cot_ref, load_sem.at[frames + 1]))
    for load in reversed(loads[:frames]):
        load.start()
    for load in loads[frames:]:
        load.start()
    for d in range(1, n_ch):
        pl.semaphore_signal(pltpu.get_barrier_semaphore(), inc=1,
                            device_id=(ctx, lax.rem(ch + d, n_ch)), device_id_type=MESH)
    for d in range(1, n_ctx):
        pl.semaphore_signal(pltpu.get_barrier_semaphore(), inc=1,
                            device_id=(lax.rem(ctx + d, n_ctx), ch), device_id_type=MESH)
    pl.semaphore_wait(pltpu.get_barrier_semaphore(), n_ch + n_ctx - 2)

    ways = ((0, 1), (1, -1))
    last = frames - 1

    def inside(place):
        return (place >= 0) & (place < n_ch)

    def hop(way, sign, d, s):
        chunk = ch - sign if d == 2 else ch
        return pltpu.make_async_remote_copy(
            src_ref=xg.at[s, chunk], dst_ref=xg.at[s, chunk],
            send_sem=gat_send.at[way, d - 1, s], recv_sem=gat_recv.at[way, d - 1, s],
            device_id=(ctx, ch + sign if d == 2 else ch + sign * d), device_id_type=MESH)

    def landing(way, sign, d, s):
        chunk = ch - sign * d
        return pltpu.make_async_remote_copy(
            src_ref=xg.at[s, chunk], dst_ref=xg.at[s, chunk],
            send_sem=gat_send.at[way, d - 1, s], recv_sem=gat_recv.at[way, d - 1, s],
            device_id=(ctx, ch - sign), device_id_type=MESH)

    def hops(sign, d):
        return inside(ch - sign) & inside(ch + sign) if d == 2 else inside(ch + sign * d)

    direct = [1] + list(range(3, n_ch))
    for s in reversed(range(frames)):
        loads[s].wait()
        for d in direct:
            for way, sign in ways:
                @pl.when(hops(sign, d))
                def _(way=way, sign=sign, d=d, s=s):
                    hop(way, sign, d, s).start()
    loads[frames].wait()
    wt[...] = jnp.transpose(w_ref[...].reshape(rows, width))
    for s in reversed(range(frames)):
        for way, sign in ways:
            @pl.when(inside(ch - sign))
            def _(way=way, sign=sign, s=s):
                landing(way, sign, 1, s).wait_recv()

            @pl.when(hops(sign, 2))
            def _(way=way, sign=sign, s=s):
                hop(way, sign, 2, s).start()

    def gathered(s):
        for d in range(2, n_ch):
            for way, sign in ways:
                @pl.when(inside(ch - sign * d))
                def _(way=way, sign=sign, d=d):
                    landing(way, sign, d, s).wait_recv()

    masks = edge_masks()

    def convolve(s):
        x = xg[s].reshape(width, CELLS)
        for k in range(3):
            prod = jnp.dot(w_ref[9 * k : 9 * k + 9].reshape(9 * own, width), x,
                           preferred_element_type=f32)
            total = None
            for spot, (r, c) in enumerate(offsets):
                part = moved(prod[spot * own : (spot + 1) * own], r, c, masks)
                total = part if total is None else total + part
            terms[s, k] = total

    def fwd_copy():
        return pltpu.make_async_remote_copy(
            src_ref=fwd_out, dst_ref=fwd_in, send_sem=halo_send.at[0], recv_sem=halo_recv.at[0],
            device_id=(lax.rem(ctx + 1, n_ctx), ch), device_id_type=MESH)

    def bwd_copy():
        return pltpu.make_async_remote_copy(
            src_ref=bwd_out, dst_ref=bwd_in, send_sem=halo_send.at[1], recv_sem=halo_recv.at[1],
            device_id=(lax.rem(ctx + n_ctx - 1, n_ctx), ch), device_id_type=MESH)

    gathered(last)
    convolve(last)
    fwd_out[0] = (terms[last, 1] + terms[last, 2]).astype(bf16)
    fwd_out[1] = terms[last, 2].astype(bf16)

    @pl.when(ctx + 1 < n_ctx)
    def _():
        fwd_copy().start()

    for s in reversed(range(last)):
        gathered(s)
        convolve(s)
    loads[frames + 1].wait()

    def same(a, b):
        return (ids_ref[a] == ids_ref[b]).astype(f32)

    base = ctx * frames
    top = n_ctx * frames - 1

    def joined(s):
        low = jnp.maximum(base + s - 1, 0) if s == 0 else base + s - 1
        return same(low, base + s)

    def slopes(s, both, late):
        gate = joined(s)
        for odd in range(2):
            if odd == 0:
                pre = terms[s, 0] + gate * both
            else:
                pre = terms[s, 0] + terms[s, 1] + gate * late
            sig = jax.nn.sigmoid(pre)
            slope = sig * (1.0 + pre * (1.0 - sig))
            grads[2 * s + odd] = (cot_ref[2 * s + odd].astype(f32) * slope).astype(bf16)

    for s in range(1, frames):
        slopes(s, terms[s - 1, 1] + terms[s - 1, 2], terms[s - 1, 2])

    @pl.when(ctx > 0)
    def _():
        fwd_copy().wait_recv()

    @pl.when(ctx == 0)
    def _():
        fwd_in[...] = jnp.zeros_like(fwd_in)

    slopes(0, fwd_in[0].astype(f32), fwd_in[1].astype(f32))
    bwd_out[0] = grads[0]
    bwd_out[1] = (grads[0].astype(f32) + grads[1].astype(f32)).astype(bf16)

    @pl.when(ctx > 0)
    def _():
        bwd_copy().start()

    def x_copy(way, sign, d, s):
        return pltpu.make_async_remote_copy(
            src_ref=sx.at[s, ch + sign * d], dst_ref=rx.at[s, way, d - 1],
            send_sem=x_send.at[s, way, d - 1], recv_sem=x_recv.at[s, way, d - 1],
            device_id=(ctx, ch + sign if d == 2 else ch + sign * d), device_id_type=MESH)

    def x_landing(way, sign, d, s):
        return pltpu.make_async_remote_copy(
            src_ref=rx.at[s, way, d - 1], dst_ref=rx.at[s, way, d - 1],
            send_sem=x_send.at[s, way, d - 1], recv_sem=x_recv.at[s, way, d - 1],
            device_id=(ctx, ch - sign), device_id_type=MESH)

    def x_start(s):
        for d in range(2, n_ch):
            for way, sign in ways:
                @pl.when(inside(ch + sign * d))
                def _(way=way, sign=sign, d=d):
                    x_copy(way, sign, d, s).start()

    def x_relay(s):
        for way, sign in ways:
            @pl.when(hops(sign, 2))
            def _(way=way, sign=sign):
                x_landing(way, sign, 2, s).wait_recv()
                both = sx[s, ch + sign].astype(f32) + rx[s, way, 1].astype(f32)
                sx[s, ch + sign] = both.astype(bf16)

            @pl.when(inside(ch + sign))
            def _(way=way, sign=sign):
                x_copy(way, sign, 1, s).start()

    half = n_ctx // 2
    side, pair_at = lax.rem(ctx, 2), ctx // 2

    def core_copy(q):
        return pltpu.make_async_remote_copy(
            src_ref=sw.at[1 - side, q], dst_ref=rc.at[q],
            send_sem=c_send.at[q], recv_sem=c_recv.at[q],
            device_id=(ctx + 1 - 2 * side, ch), device_id_type=MESH)

    def w_copy(d):
        q = lax.rem(pair_at + d, half)
        return pltpu.make_async_remote_copy(
            src_ref=sw.at[side, q], dst_ref=rw.at[d],
            send_sem=w_send.at[d], recv_sem=w_recv.at[d],
            device_id=(2 * q + side, ch), device_id_type=MESH)

    for s in range(frames):
        if s == last:
            @pl.when(ctx + 1 < n_ctx)
            def _():
                bwd_copy().wait_recv()

            @pl.when(ctx + 1 == n_ctx)
            def _():
                bwd_in[...] = jnp.zeros_like(bwd_in)

            after, pair = bwd_in[0].astype(f32), bwd_in[1].astype(f32)
            gate = same(base + s, jnp.minimum(base + s + 1, top))
        else:
            after = grads[2 * s + 2].astype(f32)
            pair = after + grads[2 * s + 3].astype(f32)
            gate = same(base + s, base + s + 1)
        odd = grads[2 * s + 1].astype(f32)
        groups = [grads[2 * s].astype(f32) + odd, odd + gate * after, gate * pair]
        for k in range(3):
            for spot, (r, c) in enumerate(offsets):
                tap = 9 * k + spot
                stack[s, tap * own : (tap + 1) * own] = moved(groups[k], -r, -c, masks).astype(bf16)
        dx = jnp.dot(wt[...], stack[s], preferred_element_type=f32)
        sx[s] = dx.reshape(n_ch, own, CELLS).astype(bf16)
        x_start(s)
        if s > 0:
            x_relay(s - 1)
        x = xg[s].reshape(width, CELLS)
        dw = lax.dot_general(x, stack[s], (((1,), (1,)), ((), ())), preferred_element_type=f32)
        if s == 0:
            acc[...] = dw
        elif s < last:
            acc[...] += dw
        else:
            full = (acc[...] + dw if frames > 1 else dw).reshape(half, 2, share, rows)
            for p in range(2):
                sw[p] = full[:, p].astype(bf16)
    for q in range(half):
        core_copy(q).start()
    for q in range(half):
        core_copy(q).wait_recv()
        sw[side, q] = (sw[side, q].astype(f32) + rc[q].astype(f32)).astype(bf16)
    for d in range(1, half):
        w_copy(d).start()
    x_relay(last)

    for s in range(frames):
        terms[s, 0] = sx[s, ch].astype(f32)
        for d in reversed(direct):
            for way, sign in ways:
                @pl.when(inside(ch - sign * d))
                def _(way=way, sign=sign, d=d, s=s):
                    x_landing(way, sign, d, s).wait_recv()
                    terms[s, 0] += rx[s, way, d - 1].astype(f32)

        gl_ref[s] = terms[s, 0].astype(bf16)
    total = sw[side, pair_at].astype(f32)
    for d in range(1, half):
        w_copy(d).wait_recv()
        total = total + rw[d].astype(f32)
    for tap in range(gw_ref.shape[0]):
        gw_ref[tap] = total[:, tap * own : (tap + 1) * own]

    for s in range(frames):
        for d in range(1, n_ch):
            for way, sign in ways:
                @pl.when(hops(sign, d))
                def _(way=way, sign=sign, d=d, s=s):
                    hop(way, sign, d, s).wait_send()

                @pl.when(inside(ch + sign * d))
                def _(way=way, sign=sign, d=d, s=s):
                    x_copy(way, sign, d, s).wait_send()

    @pl.when(ctx + 1 < n_ctx)
    def _():
        fwd_copy().wait_send()

    @pl.when(ctx > 0)
    def _():
        bwd_copy().wait_send()

    for q in range(half):
        core_copy(q).wait_send()
    for d in range(1, half):
        w_copy(d).wait_send()


def on_device(n_ctx, n_ch, latent, cotangent, weight, clip_ids):
    frames, own = latent.shape[:2]
    taps, _, width = weight.shape
    rows, share = taps * own, width // n_ctx
    bf16, f32 = jnp.bfloat16, jnp.float32
    dma = pltpu.SemaphoreType.DMA
    vmem = pl.BlockSpec(memory_space=pltpu.VMEM)
    hbm = pl.BlockSpec(memory_space=pltpu.HBM)
    grad_latent, grad_weight = pl.pallas_call(
        functools.partial(kernel, n_ctx, n_ch),
        out_shape=(
            jax.ShapeDtypeStruct(latent.shape, bf16),
            jax.ShapeDtypeStruct((taps, share, own), f32),
        ),
        in_specs=[pl.BlockSpec(memory_space=pltpu.SMEM), hbm, hbm, hbm],
        out_specs=(vmem, vmem),
        scratch_shapes=[
            pltpu.VMEM(weight.shape, bf16),
            pltpu.VMEM(cotangent.shape, bf16),
            pltpu.VMEM((frames, n_ch, own, CELLS), bf16),
            pltpu.VMEM((width, rows), bf16),
            pltpu.VMEM((frames, 3, own, CELLS), f32),
            pltpu.VMEM((2, own, CELLS), bf16),
            pltpu.VMEM((2, own, CELLS), bf16),
            pltpu.VMEM((2, own, CELLS), bf16),
            pltpu.VMEM((2, own, CELLS), bf16),
            pltpu.VMEM((2 * frames, own, CELLS), bf16),
            pltpu.VMEM((frames, rows, CELLS), bf16),
            pltpu.VMEM((frames, n_ch, own, CELLS), bf16),
            pltpu.VMEM((frames, 2, n_ch - 1, own, CELLS), bf16),
            pltpu.VMEM((width, rows), f32),
            pltpu.VMEM((2, n_ctx // 2, share, rows), bf16),
            pltpu.VMEM((n_ctx // 2, share, rows), bf16),
            pltpu.VMEM((n_ctx // 2, share, rows), bf16),
            dma((frames + 2,)),
            dma((2, n_ch - 1, frames)),
            dma((2, n_ch - 1, frames)),
            dma((2,)),
            dma((2,)),
            dma((frames, 2, n_ch - 1)),
            dma((frames, 2, n_ch - 1)),
            dma((n_ctx // 2,)),
            dma((n_ctx // 2,)),
            dma((n_ctx // 2,)),
            dma((n_ctx // 2,)),
        ],
        compiler_params=pltpu.CompilerParams(
            collective_id=0, has_side_effects=True, vmem_limit_bytes=64000 * 1024
        ),
    )(clip_ids, latent, cotangent, weight)
    return grad_latent, jnp.swapaxes(grad_weight, 1, 2)


def solution(mesh):
    placed = (P("ctx", "ch", None), P("ctx", "ch", None), P(None, "ch", None), P())
    return jax.shard_map(
        functools.partial(on_device, mesh.shape["ctx"], mesh.shape["ch"]),
        mesh=mesh,
        in_specs=placed,
        out_specs=(P("ctx", "ch", None), P(None, "ch", "ctx")),
        check_vma=False,
    )
```
